256 devices in a mesh: seq: 16 (over y, x), exp: 16 (over z, core), dp: 1.
Axes of the slice: x: 4, y: 4, z: 8, core: 2. Of those that a mesh axis runs over, the one named last changes fastest.
Arguments:
- tokens: bfloat16 [16, 64, 64, 1280], P(('dp', 'exp'), 'seq'), may hold values from -6 to 6
- expert_ids: int32 [16, 64, 64, 1], P(('dp', 'exp'), 'seq'), may hold values from 0 to 31; in each aligned block of 256 rows (0 to 255, 256 to 511, ..., all dimensions but the last counted through in order) at most 10 rows name the same one
- gate_values: float32 [16, 64, 64], P(('dp', 'exp'), 'seq'), may hold values from 0.25 to 1
- mixer_gain: float32 [1280], replicated, may hold values from 0.1 to 1.9
- expert_gain: float32 [1280], replicated, may hold values from 0.1 to 1.9
- conv_weight: float32 [3, 3, 1280], replicated, may hold values from -2 to 2
- conv_bias: float32 [1280], replicated, may hold values from -3 to 3
- w_in: bfloat16 [32, 1280, 5120], P('exp', None, 'seq'), may hold values from -0.15625 to 0.15625
- b_in: float32 [32, 5120], P('exp', 'seq'), may hold values from -3 to 3
- w_out: bfloat16 [32, 5120, 1280], P('exp', 'seq'), may hold values from -0.078125 to 0.078125
- b_out: float32 [32, 1280], P('exp'), may hold values from -3 to 3
Outputs:
- result: bfloat16 [16, 64, 64, 1280], P(('dp', 'exp'), 'seq')
The draws below stay inside these ranges and needn't reach their ends.
Inputs may be any that keep to these rules, and one draw needn't show every extreme that they name: `expert_ids`: among the 256 patches of one image's block of 4 rows (rows k * 4 to k * 4 + 3), no expert is chosen more than 10 times, and in every draw some expert is chosen exactly 10 times in some block.
All inputs are finite; a program needn't handle non-finite values.
Results may differ from the reference program's by a relative error of at most 0.006.
Values may be sent and summed in bfloat16 or wider, within the bound.
No kernel may reach another device: no remote copies, remote signals or barrier semaphores. Data moves between devices by JAX's collectives and lax.ppermute only.
A program may use at most 128 MiB of HBM per device.

```python
import math
import jax
import jax.numpy as jnp
import numpy as np
from jax import lax

D = 1280
FF = 5120
WIDTH = 64
EXPERTS = 32
HEIGHT = 64
IMAGES = 16
TOK_DEV = 256
CAP = 10
N_SEQ = 16


def steps_of(stream_key, extent, split, low, largest):
    level = 1.0
    for dim, shards_of in split:
        heights = jax.random.uniform(jax.random.fold_in(jax.random.fold_in(stream_key, 6), dim), (shards_of,), jnp.float32, low / len(split), largest / len(split))
        level = level * jnp.repeat(jnp.exp(heights), extent[dim] // shards_of).reshape((-1,) + (1,) * (len(extent) - 1 - dim))
    return level


def shared_out(key, own, number, rows, amount, top, limit, slope):
    sequence = jax.random.permutation(key, amount)
    packed, usual = load_shares(amount, rows * top, limit, slope, True), load_shares(amount, rows * top, limit, slope, False)
    places = jnp.arange(amount)

    def named(tallies, rotation):
        used = int((tallies > 0).sum())
        fixed = max(1, used // 4)
        passed = fixed + (places - fixed + rotation * (used - fixed)) % max(1, amount - fixed)
        return jnp.zeros((amount,), jnp.int32).at[sequence[jnp.where(places < fixed, places, passed)]].set(jnp.asarray(tallies, jnp.int32))

    tallies = jnp.where(number % 4 == 0, named(packed, number // 4), named(usual, number - number // 4 - 1))
    mixed = jax.random.permutation(jax.random.fold_in(own, 3), amount)
    source_of, taker = mixed[0:amount // 2 * 2:2], mixed[1:amount // 2 * 2:2]
    margin = jnp.minimum(tallies[source_of] - 1, limit - tallies[taker]) // 2
    margin = jnp.where((source_of == sequence[0]) | (taker == sequence[0]) | (tallies[taker] == 0), 0, jnp.maximum(margin, 0))
    passed = jax.random.randint(jax.random.fold_in(own, 4), (amount // 2,), 0, 1 << 20) % (margin + 1)
    tallies = tallies.at[source_of].add(-passed).at[taker].add(passed)
    labels = jnp.searchsorted(jnp.cumsum(tallies), jnp.arange(rows * top), side="right").astype(jnp.int32)
    grid = labels.reshape(top, rows).T
    grid = grid[jax.random.permutation(jax.random.fold_in(own, 1), rows)]
    rotation = jax.random.randint(jax.random.fold_in(own, 2), (rows, 1), 0, top)
    return jnp.take_along_axis(grid, (jnp.arange(top)[None, :] + rotation) % top, axis=1)


def load_shares(number_of, total, limit, skew, full):
    portions = [(1 << 20) // math.isqrt(rank ** skew) + 1 for rank in range(1, number_of + 1)]
    largest = limit if full else min(limit, max(-(-total // number_of), total * portions[0] // sum(portions)))
    least = 1 if total - largest >= number_of - 1 else 0
    given, spare = [largest] + [least] * (number_of - 1), total - largest - least * (number_of - 1)
    while spare > 0:
        candidates = [i for i in range(1, number_of) if given[i] < largest] or [i for i in range(1, number_of) if given[i] < limit]
        mass, budget = sum([portions[i] for i in candidates]), spare
        for i in candidates:
            addition = min(limit - given[i], max(1, budget * portions[i] // mass), spare)
            given[i] = given[i] + addition
            spare = spare - addition
    return np.array(given)


def normal_values(own_key, dims, deviation, most, pieces=(), kind=jnp.bfloat16):
    values = deviation * jax.random.normal(own_key, dims, jnp.float32)
    if pieces:
        values = values * steps_of(own_key, dims, pieces, -0.22, 0.18)
    return jnp.clip(values, -most, most).astype(kind)


def setup_inputs(seed: int = 0, part: int = 0) -> dict:
    keys = jax.random.split(jax.random.key(seed), 12)
    part_keys = jax.random.split(jax.random.fold_in(keys[11], part), 12)
    tokens = normal_values(part_keys[0], (IMAGES, HEIGHT, WIDTH, D), 1.0, 6.0, ((0, 16), (1, 16)))
    expert_ids_keys = jax.random.split(jax.random.fold_in(part_keys[1], 1), IMAGES * HEIGHT * WIDTH // TOK_DEV)
    expert_ids_turns = jax.random.permutation(jax.random.fold_in(part_keys[1], 3), IMAGES * HEIGHT * WIDTH // TOK_DEV)
    expert_ids = jax.vmap(lambda own, number: shared_out(jax.random.fold_in(part_keys[1], 2), own, number, TOK_DEV, EXPERTS, 1, CAP, 2))(expert_ids_keys, expert_ids_turns).reshape((IMAGES, HEIGHT, WIDTH, 1))
    gate_values = jnp.clip(jnp.exp(math.log(1.0) - 1.3862944 * jax.random.uniform(part_keys[2], (IMAGES, HEIGHT, WIDTH), jnp.float32) ** steps_of(part_keys[2], (IMAGES, HEIGHT, WIDTH), ((0, 16), (1, 16)), -0.2, 0.2)), 0.25, 1.0)
    mixer_gain = jnp.clip(1.0 + 0.18 * jax.random.normal(keys[3], (D,), jnp.float32), 0.1, 1.9)
    expert_gain = jnp.clip(1.0 + 0.18 * jax.random.normal(keys[4], (D,), jnp.float32), 0.1, 1.9)
    conv_weight = normal_values(keys[5], (3, 3, D), 9 ** -0.5, 2.0, (), jnp.float32)
    conv_bias = normal_values(keys[6], (D,), 0.5, 3.0, (), jnp.float32)
    w_in = normal_values(keys[7], (EXPERTS, D, FF), D ** -0.5, 0.15625, ((0, 16), (2, 16)))
    b_in = normal_values(keys[8], (EXPERTS, FF), 0.5, 3.0, ((0, 16), (1, 16)), jnp.float32)
    w_out = normal_values(keys[9], (EXPERTS, FF, D), FF ** -0.5, 0.078125, ((0, 16), (1, 16)))
    b_out = normal_values(keys[10], (EXPERTS, D), 0.5, 3.0, ((0, 16),), jnp.float32)
    return dict(tokens=tokens, expert_ids=expert_ids, gate_values=gate_values, mixer_gain=mixer_gain, expert_gain=expert_gain, conv_weight=conv_weight, conv_bias=conv_bias, w_in=w_in, b_in=b_in, w_out=w_out, b_out=b_out)


def normalize(values, scales):
    row_mean = lax.optimization_barrier(jnp.mean(values, axis=-1, keepdims=True))
    centred = values - row_mean
    row_var = lax.optimization_barrier(jnp.mean(centred * centred, axis=-1, keepdims=True))
    return centred * lax.rsqrt(row_var + 1e-06) * scales

def depthwise(padded, conv_weight, height, width):
    summed = padded[..., 0:height, 0:width, :] * conv_weight[0, 0]
    for row_off in range(3):
        for col_off in range(3):
            if row_off + col_off > 0:
                summed = summed + padded[..., row_off:row_off + height, col_off:col_off + width, :] * conv_weight[row_off, col_off]
    return summed

def reference(tokens, expert_ids, gate_values, mixer_gain, expert_gain, conv_weight, conv_bias, w_in, b_in, w_out, b_out):
    values = tokens.astype(jnp.float32)
    mixer_in = normalize(values, mixer_gain).astype(jnp.bfloat16).astype(jnp.float32)
    padded = jnp.pad(mixer_in, ((0, 0), (1, 1), (1, 1), (0, 0)))
    mixed = values + depthwise(padded, conv_weight, HEIGHT, WIDTH) + conv_bias
    expert_in = normalize(mixed, expert_gain).astype(jnp.bfloat16).reshape(-1, D)
    blocks = IMAGES * N_SEQ
    route_ids = expert_ids.reshape(blocks, TOK_DEV).astype(jnp.int32)
    one_hot = (route_ids[:, :, None] == jnp.arange(EXPERTS, dtype=jnp.int32)[None, None, :]).astype(jnp.int32)
    slot_rank = lax.optimization_barrier(jnp.sum(one_hot * (jnp.cumsum(one_hot, axis=1) - 1), axis=2)).astype(jnp.int32)
    slot_index = (jnp.arange(blocks, dtype=jnp.int32)[:, None] * CAP + slot_rank).reshape(-1).astype(jnp.int32)
    flat_ids = route_ids.reshape(-1)
    buffer = jnp.zeros((EXPERTS, blocks * CAP, D), jnp.bfloat16).at[flat_ids, slot_index].set(expert_in)
    piece_width = FF // N_SEQ

    def expert_pass(inputs):
        rows, first, first_bias, second, second_bias = inputs
        summed = jnp.zeros((rows.shape[0], D), jnp.float32)
        for shard in range(N_SEQ):
            low = shard * piece_width
            hidden = jnp.dot(rows, first[:, low:low + piece_width], preferred_element_type=jnp.float32) + first_bias[low:low + piece_width]
            hidden = jax.nn.gelu(hidden, approximate=False).astype(jnp.bfloat16)
            partial_sum = jnp.dot(hidden, second[low:low + piece_width], preferred_element_type=jnp.float32)
            summed = summed + partial_sum.astype(jnp.bfloat16).astype(jnp.float32)
        return (summed + second_bias).astype(jnp.bfloat16)
    expert_out = lax.map(expert_pass, (buffer, w_in, b_in, w_out, b_out))
    picked = expert_out[flat_ids, slot_index].astype(jnp.float32)
    result = mixed.reshape(-1, D) + gate_values.reshape(-1)[:, None] * picked
    return result.astype(jnp.bfloat16).reshape(IMAGES, HEIGHT, WIDTH, D)
```

```python
import functools
import jax
import jax.numpy as jnp
from jax import lax
from jax.experimental import pallas as pl
from jax.experimental.pallas import tpu as pltpu
from jax.sharding import PartitionSpec as P

SIDE = 4
AXES = ("seq", "exp")


def ring(shift, weights, exp_size):
    pairs = []
    for y in range(SIDE):
        for x in range(SIDE):
            for e in range(exp_size):
                along_x = (e % 2 == 0) == weights
                to_y = y if along_x else (y + shift) % SIDE
                to_x = (x + shift) % SIDE if along_x else x
                pairs.append(((y * SIDE + x) * exp_size + e, (to_y * SIDE + to_x) * exp_size + e))
    return pairs


def weight_groups(exp_size):
    groups = []
    for e in range(exp_size):
        for a in range(SIDE):
            if e % 2 == 0:
                groups.append([(a * SIDE + b) * exp_size + e for b in range(SIDE)])
            else:
                groups.append([(b * SIDE + a) * exp_size + e for b in range(SIDE)])
    return groups


def with_halo(cells, sides, width):
    for axis, dim in sides:
        count = lax.axis_size(axis)
        ends = count - 1
        head = lax.slice_in_dim(cells, 0, width, axis=dim)
        tail = lax.slice_in_dim(cells, cells.shape[dim] - width, cells.shape[dim], axis=dim)
        cells = jnp.concatenate(
            [
                lax.ppermute(tail, axis, [(i, (i + 1) % count) for i in range(ends)]),
                cells,
                lax.ppermute(head, axis, [((i + 1) % count, i) for i in range(ends)]),
            ],
            axis=dim,
        )
    return cells


def normalize(values, scales):
    row_mean = jnp.mean(values, axis=-1, keepdims=True)
    centred = values - row_mean
    row_var = jnp.mean(centred * centred, axis=-1, keepdims=True)
    return centred * lax.rsqrt(row_var + 1e-06) * scales


def depthwise(padded, conv_weight, height, width):
    summed = padded[..., 0:height, 0:width, :] * conv_weight[0, 0]
    for row_off in range(3):
        for col_off in range(3):
            if row_off + col_off > 0:
                summed = (
                    summed
                    + padded[..., row_off : row_off + height, col_off : col_off + width, :]
                    * conv_weight[row_off, col_off]
                )
    return summed


def gelu(v):
    return 0.5 * v * (1.0 + lax.erf(v * 0.7071067811865476))


def ffn_kernel(*refs):
    xs, wis, wos, bias, ys = refs[0:4], refs[4:8], refs[8:12], refs[12], refs[13:17]
    x_v, wi_v, wo_v, y_v, in_sem, out_sem = refs[17:]
    experts = x_v.shape[0]
    rows = xs[0].shape[1]
    units = wis[0].shape[1]
    copies = []
    for j in range(experts):
        for what, (sources, target, size) in enumerate(
            ((xs, x_v, rows), (wis, wi_v, units), (wos, wo_v, units))
        ):
            for k in range(SIDE):
                copy = pltpu.make_async_copy(
                    sources[k].at[j], target.at[j, pl.ds(k * size, size)], in_sem.at[j, what, k]
                )
                copy.start()
                copies.append(copy)
    out = []
    for j in range(experts):
        base = j * 3 * SIDE
        for copy in copies[base : base + 2 * SIDE]:
            copy.wait()
        for half in range(2):
            at = pl.ds(half * 2 * rows, 2 * rows)
            hidden = lax.dot_general(
                x_v[j, at], wi_v[j], (((1,), (1,)), ((), ())), preferred_element_type=jnp.float32
            )
            hidden = gelu(hidden + bias[j : j + 1]).astype(jnp.bfloat16)
            if half == 0:
                for copy in copies[base + 2 * SIDE : base + 3 * SIDE]:
                    copy.wait()
            part = jnp.dot(hidden, wo_v[j], preferred_element_type=jnp.float32)
            y_v[j, at] = part.astype(jnp.bfloat16)
            for k in (2 * half, 2 * half + 1):
                copy = pltpu.make_async_copy(
                    y_v.at[j, pl.ds(k * rows, rows)], ys[k].at[j], out_sem.at[j, k]
                )
                copy.start()
                out.append(copy)
    for copy in out:
        copy.wait()


def ffn(xs, wis, wos, bias):
    experts, rows, width = xs[0].shape
    units = wis[0].shape[1]
    any_spec = pl.BlockSpec(memory_space=pl.ANY)
    flops = 4 * SIDE * SIDE * experts * rows * units * width
    moved = 2 * SIDE * experts * width * (2 * rows + 2 * units)
    return pl.pallas_call(
        ffn_kernel,
        out_shape=[jax.ShapeDtypeStruct((experts, rows, width), jnp.bfloat16)] * SIDE,
        in_specs=[any_spec] * 12 + [pl.BlockSpec(memory_space=pltpu.VMEM)],
        out_specs=[any_spec] * SIDE,
        scratch_shapes=[
            pltpu.VMEM((experts, SIDE * rows, width), jnp.bfloat16),
            pltpu.VMEM((experts, SIDE * units, width), jnp.bfloat16),
            pltpu.VMEM((experts, SIDE * units, width), jnp.bfloat16),
            pltpu.VMEM((experts, SIDE * rows, width), jnp.bfloat16),
            pltpu.SemaphoreType.DMA((experts, 3, SIDE)),
            pltpu.SemaphoreType.DMA((experts, SIDE)),
        ],
        compiler_params=pltpu.CompilerParams(vmem_limit_bytes=44 * 1024 * 1024),
        cost_estimate=pl.CostEstimate(flops=flops, transcendentals=0, bytes_accessed=moved),
        name="ffn",
    )(*xs, *wis, *wos, bias)


def body(
    tokens,
    expert_ids,
    gate_values,
    mixer_gain,
    expert_gain,
    conv_weight,
    conv_bias,
    w_in,
    b_in,
    w_out,
    b_out,
):
    exp_size = lax.axis_size("exp")
    send_w = functools.partial(ring, weights=True, exp_size=exp_size)
    send_t = functools.partial(ring, weights=False, exp_size=exp_size)

    wi = jnp.swapaxes(w_in, 1, 2)
    wi_prev = lax.ppermute(wi, AXES, send_w(1))
    wi_next = lax.ppermute(wi, AXES, send_w(-1))
    wo_prev = lax.ppermute(w_out, AXES, send_w(1))
    wo_next = lax.ppermute(w_out, AXES, send_w(-1))
    wi_far = lax.ppermute(wi_prev, AXES, send_w(1))
    wo_far = lax.ppermute(wo_next, AXES, send_w(-1))
    biases = lax.all_gather(b_in, AXES, axis_index_groups=weight_groups(exp_size))
    seq = lax.axis_index("seq")
    place = jnp.where(lax.axis_index("exp") % 2 == 0, seq % SIDE, seq // SIDE)
    bias = jnp.concatenate(
        [
            sum(
                jnp.where((place + shift) % SIDE == k, biases[k], 0.0)
                for k in range(SIDE)
            )
            for shift in (0, SIDE - 1, 1, 2)
        ],
        axis=1,
    )

    row_count = tokens.shape[1]
    col_count = tokens.shape[2]
    width_d = tokens.shape[3]
    values = tokens[0].astype(jnp.float32)
    normed = normalize(values, mixer_gain).astype(jnp.bfloat16)
    rim_source = tokens[0]
    extended = with_halo(rim_source, (("seq", 0),), 1)
    rim_rows = jnp.concatenate([extended[0:1], extended[row_count + 1 : row_count + 2]], axis=0)
    rim_rows = normalize(rim_rows.astype(jnp.float32), mixer_gain).astype(jnp.bfloat16)
    extended = jnp.concatenate([rim_rows[0:1], normed, rim_rows[1:2]], axis=0)
    padded = jnp.pad(extended.astype(jnp.float32), ((0, 0), (1, 1), (0, 0)))
    mixed = values + depthwise(padded, conv_weight, row_count, col_count) + conv_bias
    tok_rows = row_count * col_count
    expert_in = normalize(mixed, expert_gain).astype(jnp.bfloat16).reshape(tok_rows, width_d)
    per_device = w_in.shape[0]
    holders = lax.axis_size("exp")
    experts = per_device * holders
    slot_count = 5 * tok_rows // (4 * experts)
    route_ids = expert_ids.reshape(tok_rows)
    one_hot = (route_ids[:, None] == jnp.arange(experts, dtype=jnp.int32)[None, :]).astype(
        jnp.float32
    )
    positions = jnp.arange(tok_rows, dtype=jnp.int32)
    below_mask = (positions[:, None] > positions[None, :]).astype(jnp.float32)
    earlier = jnp.dot(below_mask, one_hot, precision=lax.Precision.HIGHEST)
    slot_rank = jnp.sum(earlier * one_hot, axis=1).astype(jnp.int32)
    column = (
        route_ids // per_device * slot_count + slot_rank
    ) * per_device + route_ids % per_device
    dispatch_mask = (
        column[:, None] == jnp.arange(experts * slot_count, dtype=jnp.int32)[None, :]
    ).astype(jnp.bfloat16)
    dispatched = jnp.einsum(
        "tk,td->kd", dispatch_mask, expert_in, preferred_element_type=jnp.float32
    ).astype(jnp.bfloat16)
    dispatched = dispatched.reshape(holders, slot_count, per_device, width_d)
    received = lax.all_to_all(dispatched, "exp", split_axis=0, concat_axis=0, tiled=True)
    rows = jnp.transpose(received, (2, 1, 0, 3)).reshape(per_device, slot_count * holders, width_d)
    x_prev = lax.ppermute(rows, AXES, send_t(1))
    x_next = lax.ppermute(rows, AXES, send_t(-1))
    x_far = lax.ppermute(rows, AXES, send_t(2))
    y_own, y_prev, y_next, y_far = ffn(
        (rows, x_prev, x_next, x_far),
        (wi, wi_prev, wi_next, wi_far),
        (w_out, wo_prev, wo_next, wo_far),
        bias,
    )
    parts = (
        y_own,
        lax.ppermute(y_prev, AXES, send_t(-1)),
        lax.ppermute(y_next, AXES, send_t(1)),
        lax.ppermute(y_far, AXES, send_t(2)),
    )
    summed = sum(part.astype(jnp.float32) for part in parts)
    back = (summed + b_out[:, None]).astype(jnp.bfloat16)
    back = jnp.transpose(
        back.reshape(per_device, slot_count, holders, width_d), (2, 1, 0, 3)
    )
    returned = lax.all_to_all(back, "exp", split_axis=0, concat_axis=0, tiled=True).reshape(
        experts * slot_count, width_d
    )
    combined = jnp.dot(dispatch_mask, returned, preferred_element_type=jnp.float32)
    result = mixed.reshape(tok_rows, width_d) + gate_values.reshape(tok_rows)[:, None] * combined
    return result.astype(jnp.bfloat16).reshape(tokens.shape)


def solution(mesh):
    in_specs = (
        P(("dp", "exp"), "seq", None, None),
        P(("dp", "exp"), "seq", None, None),
        P(("dp", "exp"), "seq", None),
        P(),
        P(),
        P(),
        P(),
        P("exp", None, "seq"),
        P("exp", "seq"),
        P("exp", "seq", None),
        P("exp", None),
    )
    out_specs = P(("dp", "exp"), "seq", None, None)
    return jax.shard_map(body, mesh=mesh, in_specs=in_specs, out_specs=out_specs, check_vma=False)
```

```python
import functools
import jax
import jax.numpy as jnp
import numpy as np
from jax import lax
from jax.experimental import pallas as pl
from jax.experimental.pallas import tpu as pltpu
from jax.sharding import PartitionSpec as P

SIDE = 4
AXES = ("seq", "exp")
VMEM = pl.BlockSpec(memory_space=pltpu.VMEM)
ANY = pl.BlockSpec(memory_space=pl.ANY)
HBM = pl.BlockSpec(memory_space=pltpu.HBM)
PIECES = 3
MIX_COST = 60000
ADD_COST = 16000
EXTRA = 16


def ring(shift, weights, exp_size):
    pairs = []
    for y in range(SIDE):
        for x in range(SIDE):
            for e in range(exp_size):
                along_x = (e % 2 == 0) == weights
                to_y = y if along_x else (y + shift) % SIDE
                to_x = (x + shift) % SIDE if along_x else x
                pairs.append(((y * SIDE + x) * exp_size + e, (to_y * SIDE + to_x) * exp_size + e))
    return pairs


def tables(holders, slots):
    pick = np.zeros((2, 2 * holders * slots, 4 * holders * slots), np.float32)
    for half in range(2):
        for j in range(2):
            for s in range(holders):
                for c in range(slots):
                    row = (j * holders + s) * slots + c
                    pick[half, row, s * 4 * slots + half * 2 * slots + j * slots + c] = 1.0
    return pick.astype(jnp.bfloat16), np.swapaxes(pick, 1, 2).astype(jnp.bfloat16)


def append_kernel(wi_ref, bias_ref, out_ref, rows_v, sems):
    experts, units, width = wi_ref.shape
    copies = []
    for j in range(experts):
        copy = pltpu.make_async_copy(wi_ref.at[j], out_ref.at[j, pl.ds(0, units)], sems.at[j])
        copy.start()
        copies.append(copy)
    rows_v[...] = jnp.zeros_like(rows_v)
    for j in range(experts):
        rows_v[j, 0:1, 0:units] = bias_ref[j : j + 1]
    for j in range(experts):
        left = rows_v[j, 0:1]
        for p in range(PIECES):
            piece = left.astype(jnp.bfloat16).astype(jnp.float32)
            left = left - piece
            for k in range(SIDE):
                row = PIECES * k + p
                rows_v[j, row : row + 1] = pltpu.roll(piece, k * units, 1) if k else piece
        out_ref[j, units : units + EXTRA] = rows_v[j].astype(jnp.bfloat16)
    for copy in copies:
        copy.wait()


def append_rows(wi, bias):
    experts, units, width = wi.shape
    return pl.pallas_call(
        append_kernel,
        out_shape=jax.ShapeDtypeStruct((experts, units + EXTRA, width), jnp.bfloat16),
        in_specs=[ANY, VMEM],
        out_specs=VMEM,
        scratch_shapes=[
            pltpu.VMEM((experts, EXTRA, width), jnp.float32),
            pltpu.SemaphoreType.DMA((experts,)),
        ],
        compiler_params=pltpu.CompilerParams(vmem_limit_bytes=8 * 1024 * 1024),
        name="append_rows",
    )(wi, bias)


def normalize(values, scales):
    row_mean = jnp.mean(values, axis=-1, keepdims=True)
    centred = values - row_mean
    row_var = jnp.mean(centred * centred, axis=-1, keepdims=True)
    return centred * lax.rsqrt(row_var + 1e-06) * scales


def gelu(v):
    return 0.5 * v * (1.0 + lax.erf(v * 0.7071067811865476))


def mix_kernel(
    holders,
    slots,
    tok_ref,
    up_ref,
    down_ref,
    ids_ref,
    mixer_gain,
    expert_gain,
    conv_weight,
    conv_bias,
    mixed_ref,
    msg_ref,
    column_ref,
    norm_v,
    in_v,
    mixed_v,
    msg_v,
    sems,
):
    rows, cols, width = tok_ref.shape
    tokens = rows * cols
    gain = mixer_gain[...].reshape(1, width)
    out_gain = expert_gain[...].reshape(1, width)
    shift = conv_bias[...].reshape(1, width)
    for r in range(rows):
        norm_v[r + 1] = normalize(tok_ref[r].astype(jnp.float32), gain).astype(jnp.bfloat16)
    norm_v[0] = normalize(up_ref[0].astype(jnp.float32), gain).astype(jnp.bfloat16)
    norm_v[rows + 1] = normalize(down_ref[0].astype(jnp.float32), gain).astype(jnp.bfloat16)
    place = lax.broadcasted_iota(jnp.int32, (cols, 1), 0)
    copies = []
    for r in range(rows):
        sums = []
        for b in range(3):
            total = None
            for a in range(3):
                term = norm_v[r + a].astype(jnp.float32) * conv_weight[a, b : b + 1]
                total = term if total is None else total + term
            sums.append(total)
        left = jnp.where(place == 0, 0.0, pltpu.roll(sums[0], 1, 0))
        right = jnp.where(place == cols - 1, 0.0, pltpu.roll(sums[2], cols - 1, 0))
        mixed = tok_ref[r].astype(jnp.float32) + shift + sums[1] + left + right
        at = pl.ds(r * cols, cols)
        mixed_v[at] = mixed
        in_v[at] = normalize(mixed, out_gain).astype(jnp.bfloat16)
    copies.append(pltpu.make_async_copy(mixed_v, mixed_ref, sems.at[0]))
    copies[0].start()
    ids = ids_ref[...]
    experts = 2 * holders
    kinds = lax.broadcasted_iota(jnp.int32, (experts, tokens), 0)
    hot = kinds == ids
    before = lax.broadcasted_iota(jnp.int32, (tokens, tokens), 0) < lax.broadcasted_iota(
        jnp.int32, (tokens, tokens), 1
    )
    earlier = jnp.dot(
        hot.astype(jnp.float32).astype(jnp.bfloat16),
        before.astype(jnp.float32).astype(jnp.bfloat16),
        preferred_element_type=jnp.float32,
    )
    rank = jnp.sum(jnp.where(hot, earlier, 0.0), axis=0, keepdims=True).astype(jnp.int32)
    holder = lax.shift_right_logical(ids, 1)
    which = ids & 1
    col = holder * (4 * slots) + which * slots + rank
    column_ref[...] = col
    at = lax.broadcasted_iota(jnp.int32, (4 * slots * holders, tokens), 0)
    pick_left = (at == col).astype(jnp.float32).astype(jnp.bfloat16)
    pick_right = (at == col + 2 * slots).astype(jnp.float32).astype(jnp.bfloat16)
    msg_v[...] = (
        jnp.dot(pick_left, in_v[:, : width // 2], preferred_element_type=jnp.float32)
        + jnp.dot(pick_right, in_v[:, width // 2 :], preferred_element_type=jnp.float32)
    ).astype(jnp.bfloat16)
    copies.append(pltpu.make_async_copy(msg_v, msg_ref, sems.at[1]))
    copies[1].start()
    for copy in copies:
        copy.wait()


def mix(holders, slots, tokens, up, down, ids, mixer_gain, expert_gain, conv_weight, conv_bias):
    rows, cols, width = tokens.shape
    size = rows * cols * width
    message = (4 * slots * holders, width // 2)
    return pl.pallas_call(
        functools.partial(mix_kernel, holders, slots),
        out_shape=[
            jax.ShapeDtypeStruct((rows * cols, width), jnp.float32),
            jax.ShapeDtypeStruct(message, jnp.bfloat16),
            jax.ShapeDtypeStruct((1, rows * cols), jnp.int32),
        ],
        in_specs=[VMEM] * 8,
        out_specs=[HBM, HBM, VMEM],
        scratch_shapes=[
            pltpu.VMEM((rows + 2, cols, width), jnp.bfloat16),
            pltpu.VMEM((rows * cols, width), jnp.bfloat16),
            pltpu.VMEM((rows * cols, width), jnp.float32),
            pltpu.VMEM(message, jnp.bfloat16),
            pltpu.SemaphoreType.DMA((2,)),
        ],
        compiler_params=pltpu.CompilerParams(vmem_limit_bytes=16 * 1024 * 1024),
        cost_estimate=pl.CostEstimate(flops=MIX_COST * size, transcendentals=0, bytes_accessed=6 * size),
        name="mix",
    )(tokens, up, down, ids, mixer_gain, expert_gain, conv_weight, conv_bias)


def ffn_kernel(count, *refs):
    wis, wos, refs = refs[0:4], refs[4:8], refs[8:]
    pick, place, refs = refs[0], refs[1], refs[2:]
    msgs, outs, refs = refs[:count], refs[count : 2 * count], refs[2 * count :]
    r_v, x_v, wi_v, wo_v, b_v, y_v, o_v, msg_sem, w_sem, b_sem, out_sem = refs
    experts, _, width = x_v.shape
    rows = pick.shape[1] // experts
    units = wos[0].shape[1]
    half = width // 2
    msg_copies = []
    for k in range(count):
        copy = pltpu.make_async_copy(msgs[k], r_v.at[k], msg_sem.at[k])
        copy.start()
        msg_copies.append(copy)
    w_copies = {}
    for j in range(experts):
        for what, (sources, target) in enumerate(((wis, wi_v), (wos, wo_v))):
            group = []
            for k in range(SIDE):
                copy = pltpu.make_async_copy(
                    sources[k].at[j, pl.ds(0, units)],
                    target.at[j, pl.ds(k * units, units)],
                    w_sem.at[j, what, k],
                )
                copy.start()
                group.append(copy)
                if what == 0:
                    copy = pltpu.make_async_copy(
                        wis[k].at[j, pl.ds(units, EXTRA)], b_v.at[j, k], b_sem.at[j, k]
                    )
                    copy.start()
                    group.append(copy)
            w_copies[j, what] = group
    for k in range(count):
        msg_copies[k].wait()
        for side in range(2):
            rows_of = jnp.dot(pick[side], r_v[k], preferred_element_type=jnp.float32).astype(
                jnp.bfloat16
            )
            for j in range(experts):
                x_v[j, k * rows : (k + 1) * rows, side * half : (side + 1) * half] = rows_of[
                    j * rows : (j + 1) * rows
                ]
    for j in range(experts):
        for copy in w_copies[j, 0]:
            copy.wait()
        hidden = lax.dot_general(
            x_v[j], wi_v[j], (((1,), (1,)), ((), ())), preferred_element_type=jnp.float32
        )
        bias = sum(
            jnp.sum(
                b_v[j, k].astype(jnp.float32)[PIECES * k : PIECES * (k + 1)], axis=0, keepdims=True
            )
            for k in range(SIDE)
        )
        hidden = gelu(hidden + bias).astype(jnp.bfloat16)
        for copy in w_copies[j, 1]:
            copy.wait()
        part = jnp.dot(hidden, wo_v[j], preferred_element_type=jnp.float32).astype(jnp.bfloat16)
        for k in range(count):
            y_v[k, j * rows : (j + 1) * rows] = part[k * rows : (k + 1) * rows]
    out_copies = []
    for k in range(count):
        o_v[k] = (
            jnp.dot(place[0], y_v[k, :, :half], preferred_element_type=jnp.float32)
            + jnp.dot(place[1], y_v[k, :, half:], preferred_element_type=jnp.float32)
        ).astype(jnp.bfloat16)
        copy = pltpu.make_async_copy(o_v.at[k], outs[k], out_sem.at[k])
        copy.start()
        out_copies.append(copy)
    for copy in out_copies:
        copy.wait()


def ffn(msgs, wis, wos, pick, place):
    experts, units, width = wos[0].shape
    count = len(msgs)
    rows = pick.shape[1] // experts
    total = count * rows
    flops = 4 * experts * total * SIDE * units * width
    moved = 2 * experts * width * (4 * total + 2 * SIDE * units)
    return pl.pallas_call(
        functools.partial(ffn_kernel, count),
        out_shape=[jax.ShapeDtypeStruct(msgs[0].shape, jnp.bfloat16)] * count,
        in_specs=[ANY] * 8 + [VMEM] * 2 + [ANY] * count,
        out_specs=[ANY] * count,
        scratch_shapes=[
            pltpu.VMEM((count,) + msgs[0].shape, jnp.bfloat16),
            pltpu.VMEM((experts, total, width), jnp.bfloat16),
            pltpu.VMEM((experts, SIDE * units, width), jnp.bfloat16),
            pltpu.VMEM((experts, SIDE * units, width), jnp.bfloat16),
            pltpu.VMEM((experts, SIDE, EXTRA, width), jnp.bfloat16),
            pltpu.VMEM((count, experts * rows, width), jnp.bfloat16),
            pltpu.VMEM((count,) + msgs[0].shape, jnp.bfloat16),
            pltpu.SemaphoreType.DMA((count,)),
            pltpu.SemaphoreType.DMA((experts, 2, SIDE)),
            pltpu.SemaphoreType.DMA((experts, SIDE)),
            pltpu.SemaphoreType.DMA((count,)),
        ],
        compiler_params=pltpu.CompilerParams(vmem_limit_bytes=32 * 1024 * 1024),
        cost_estimate=pl.CostEstimate(flops=2 * flops, transcendentals=0, bytes_accessed=moved),
        name="ffn",
    )(*wis, *wos, pick, place, *msgs)


def add_kernel(a_ref, b_ref, c_ref, out_ref):
    out_ref[...] = a_ref[...].astype(jnp.float32) + b_ref[...].astype(jnp.float32) + c_ref[...]


def add_parts(a, b, c):
    return pl.pallas_call(
        add_kernel,
        out_shape=jax.ShapeDtypeStruct(a.shape, jnp.float32),
        in_specs=[VMEM] * 3,
        out_specs=VMEM,
        cost_estimate=pl.CostEstimate(
            flops=ADD_COST * a.size, transcendentals=0, bytes_accessed=12 * a.size
        ),
        compiler_params=pltpu.CompilerParams(vmem_limit_bytes=16 * 1024 * 1024),
        name="add_parts",
    )(a, b, c)


def combine_kernel(mixed_ref, gate_ref, col_ref, msg_ref, out_ref):
    tokens, width = mixed_ref.shape
    gate = gate_ref[...]
    count = msg_ref.shape[0]
    step = count // 32
    at_col = lax.broadcasted_iota(jnp.int32, (tokens, count), 1)
    for side in range(2):
        at = slice(side * width // 2, (side + 1) * width // 2)
        pick = at_col == col_ref[...] + step * side
        picked = jnp.dot(
            pick.astype(jnp.float32).astype(jnp.bfloat16),
            msg_ref[...],
            preferred_element_type=jnp.float32,
        )
        out_ref[:, at] = (mixed_ref[:, at] + gate * picked).astype(jnp.bfloat16)


def combine(mixed, gate, columns, msg):
    return pl.pallas_call(
        combine_kernel,
        out_shape=jax.ShapeDtypeStruct(mixed.shape, jnp.bfloat16),
        in_specs=[VMEM] * 4,
        out_specs=VMEM,
        compiler_params=pltpu.CompilerParams(vmem_limit_bytes=16 * 1024 * 1024),
        name="combine",
    )(mixed, gate, columns, msg)


def body(
    tokens,
    expert_ids,
    gate_values,
    mixer_gain,
    expert_gain,
    conv_weight,
    conv_bias,
    w_in,
    b_in,
    w_out,
    b_out,
):
    exp_size = lax.axis_size("exp")
    seq_size = lax.axis_size("seq")
    send_w = functools.partial(ring, weights=True, exp_size=exp_size)
    send_t = functools.partial(ring, weights=False, exp_size=exp_size)
    _, row_count, col_count, width = tokens.shape
    tok_rows = row_count * col_count
    per_device = w_in.shape[0]
    slots = 5 * tok_rows // (4 * per_device * exp_size)

    together = lax.optimization_barrier
    head, tail = tokens[0, 0:1], tokens[0, row_count - 1 : row_count]
    wi = append_rows(jnp.swapaxes(w_in, 1, 2), b_in)
    head, tail, wo = together((head, tail, w_out))
    up = lax.ppermute(tail, "seq", [(i, i + 1) for i in range(seq_size - 1)])
    down = lax.ppermute(head, "seq", [(i + 1, i) for i in range(seq_size - 1)])
    wo_prev = lax.ppermute(wo, AXES, send_w(1))
    wo_next = lax.ppermute(wo, AXES, send_w(-1))
    wi_prev = lax.ppermute(wi, AXES, send_w(1))
    wi_next = lax.ppermute(wi, AXES, send_w(-1))
    wo_far = lax.ppermute(wo_prev, AXES, send_w(1))
    wi_far = lax.ppermute(wi_next, AXES, send_w(-1))
    mixed, msg, columns = mix(
        exp_size,
        slots,
        tokens[0],
        up,
        down,
        expert_ids.reshape(1, tok_rows),
        mixer_gain,
        expert_gain,
        conv_weight,
        conv_bias,
    )

    def exchange(msg):
        shape = msg.shape
        msg = msg.reshape(exp_size, shape[0] // exp_size, shape[1])
        return lax.all_to_all(msg, "exp", split_axis=0, concat_axis=0, tiled=True).reshape(shape)

    msg = exchange(msg)
    msg_far = lax.ppermute(msg, AXES, send_t(2))
    msg_prev = lax.ppermute(msg, AXES, send_t(1))
    msg_next = lax.ppermute(msg, AXES, send_t(-1))
    weights = ((wi, wi_prev, wi_next, wi_far), (wo, wo_prev, wo_next, wo_far))
    lists = tables(exp_size, slots)
    (own,) = ffn((msg,), *weights, *lists)
    msg_far, own = together((msg_far, own))
    (far,) = ffn((msg_far,), *weights, *lists)
    msg_prev, msg_next, far = together((msg_prev, msg_next, far))
    prev, nxt = ffn((msg_prev, msg_next), *weights, *lists)
    far = lax.ppermute(far, AXES, send_t(2))
    prev = lax.ppermute(prev, AXES, send_t(-1))
    nxt = lax.ppermute(nxt, AXES, send_t(1))
    shift = jnp.transpose(b_out.reshape(per_device, 2, width // 2), (1, 0, 2))
    shift = jnp.broadcast_to(shift[None, :, :, None], (exp_size, 2, per_device, slots, width // 2))
    early = add_parts(own, far, shift.reshape(own.shape))
    back = (early + prev.astype(jnp.float32) + nxt.astype(jnp.float32)).astype(jnp.bfloat16)
    back = exchange(back)
    result = combine(mixed, gate_values.reshape(tok_rows, 1), columns.reshape(tok_rows, 1), back)
    return result.reshape(tokens.shape)


def solution(mesh):
    in_specs = (
        P(("dp", "exp"), "seq", None, None),
        P(("dp", "exp"), "seq", None, None),
        P(("dp", "exp"), "seq", None),
        P(),
        P(),
        P(),
        P(),
        P("exp", None, "seq"),
        P("exp", "seq"),
        P("exp", "seq", None),
        P("exp", None),
    )
    out_specs = P(("dp", "exp"), "seq", None, None)
    return jax.shard_map(body, mesh=mesh, in_specs=in_specs, out_specs=out_specs, check_vma=False)
```

```python
import functools
import jax
import jax.numpy as jnp
import numpy as np
from jax import lax
from jax.experimental import pallas as pl
from jax.experimental.pallas import tpu as pltpu
from jax.sharding import PartitionSpec as P

SIDE = 4
AXES = ("seq", "exp")
VMEM = pl.BlockSpec(memory_space=pltpu.VMEM)
ANY = pl.BlockSpec(memory_space=pl.ANY)
HBM = pl.BlockSpec(memory_space=pltpu.HBM)
MIX_COST = 60000


def ring(shift, weights, exp_size):
    pairs = []
    for y in range(SIDE):
        for x in range(SIDE):
            for e in range(exp_size):
                along_x = (e % 2 == 0) == weights
                to_y = y if along_x else (y + shift) % SIDE
                to_x = (x + shift) % SIDE if along_x else x
                pairs.append(((y * SIDE + x) * exp_size + e, (to_y * SIDE + to_x) * exp_size + e))
    return pairs


def weight_groups(exp_size):
    groups = []
    for e in range(exp_size):
        for a in range(SIDE):
            if e % 2 == 0:
                groups.append([(a * SIDE + b) * exp_size + e for b in range(SIDE)])
            else:
                groups.append([(b * SIDE + a) * exp_size + e for b in range(SIDE)])
    return groups


def chunk_sizes(slots):
    second = (slots * 3 // 5) // 2 * 2
    return slots - second, second


def unpack_table(holders, slots):
    pick = np.zeros((2, 2 * holders * slots, 4 * holders * slots), np.float32)
    chunks = chunk_sizes(slots)
    for half in range(2):
        row = 0
        for j in range(2):
            for k, n in enumerate(chunks):
                for s in range(holders):
                    for c in range(n):
                        slot = c + k * chunks[0]
                        pick[half, row, s * 4 * slots + half * 2 * slots + j * slots + slot] = 1.0
                        row += 1
    return pick.astype(jnp.bfloat16)


def pack_table(holders, n):
    place = np.zeros((2, 4 * holders * n, 2 * holders * n), np.float32)
    for half in range(2):
        for j in range(2):
            for s in range(holders):
                for c in range(n):
                    row = (j * holders + s) * n + c
                    place[half, s * 4 * n + half * 2 * n + j * n + c, row] = 1.0
    return place.astype(jnp.bfloat16)


def normalize(values, scales):
    row_mean = jnp.mean(values, axis=-1, keepdims=True)
    centred = values - row_mean
    row_var = jnp.mean(centred * centred, axis=-1, keepdims=True)
    return centred * lax.rsqrt(row_var + 1e-06) * scales


def gelu(v):
    return 0.5 * v * (1.0 + lax.erf(v * 0.7071067811865476))


def mix_kernel(
    holders,
    slots,
    tok_ref,
    up_ref,
    down_ref,
    ids_ref,
    mixer_gain,
    expert_gain,
    conv_weight,
    conv_bias,
    mixed_ref,
    msg_ref,
    column_ref,
    norm_v,
    in_v,
    mixed_v,
    msg_v,
    sems,
):
    rows, cols, width = tok_ref.shape
    tokens = rows * cols
    gain = mixer_gain[...].reshape(1, width)
    out_gain = expert_gain[...].reshape(1, width)
    shift = conv_bias[...].reshape(1, width)
    for r in range(rows):
        norm_v[r + 1] = normalize(tok_ref[r].astype(jnp.float32), gain).astype(jnp.bfloat16)
    norm_v[0] = normalize(up_ref[0].astype(jnp.float32), gain).astype(jnp.bfloat16)
    norm_v[rows + 1] = normalize(down_ref[0].astype(jnp.float32), gain).astype(jnp.bfloat16)
    place = lax.broadcasted_iota(jnp.int32, (cols, 1), 0)
    copies = []
    for r in range(rows):
        sums = []
        for b in range(3):
            total = None
            for a in range(3):
                term = norm_v[r + a].astype(jnp.float32) * conv_weight[a, b : b + 1]
                total = term if total is None else total + term
            sums.append(total)
        left = jnp.where(place == 0, 0.0, pltpu.roll(sums[0], 1, 0))
        right = jnp.where(place == cols - 1, 0.0, pltpu.roll(sums[2], cols - 1, 0))
        mixed = tok_ref[r].astype(jnp.float32) + shift + sums[1] + left + right
        at = pl.ds(r * cols, cols)
        mixed_v[at] = mixed
        in_v[at] = normalize(mixed, out_gain).astype(jnp.bfloat16)
    copies.append(pltpu.make_async_copy(mixed_v, mixed_ref, sems.at[0]))
    copies[0].start()
    ids = ids_ref[...]
    experts = 2 * holders
    kinds = lax.broadcasted_iota(jnp.int32, (experts, tokens), 0)
    hot = kinds == ids
    before = lax.broadcasted_iota(jnp.int32, (tokens, tokens), 0) < lax.broadcasted_iota(
        jnp.int32, (tokens, tokens), 1
    )
    earlier = jnp.dot(
        hot.astype(jnp.float32).astype(jnp.bfloat16),
        before.astype(jnp.float32).astype(jnp.bfloat16),
        preferred_element_type=jnp.float32,
    )
    rank = jnp.sum(jnp.where(hot, earlier, 0.0), axis=0, keepdims=True).astype(jnp.int32)
    holder = lax.shift_right_logical(ids, 1)
    which = ids & 1
    col = holder * (4 * slots) + which * slots + rank
    low = 0
    for k, n in enumerate(chunk_sizes(slots)):
        place_of = holder * (4 * n) + which * n + rank - low
        column_ref[k : k + 1] = jnp.where((rank >= low) & (rank < low + n), place_of, -4 * n)
        low += n
    at = lax.broadcasted_iota(jnp.int32, (4 * slots * holders, tokens), 0)
    pick_left = (at == col).astype(jnp.float32).astype(jnp.bfloat16)
    pick_right = (at == col + 2 * slots).astype(jnp.float32).astype(jnp.bfloat16)
    msg_v[...] = (
        jnp.dot(pick_left, in_v[:, : width // 2], preferred_element_type=jnp.float32)
        + jnp.dot(pick_right, in_v[:, width // 2 :], preferred_element_type=jnp.float32)
    ).astype(jnp.bfloat16)
    copies.append(pltpu.make_async_copy(msg_v, msg_ref, sems.at[1]))
    copies[1].start()
    for copy in copies:
        copy.wait()


def mix(holders, slots, tokens, up, down, ids, mixer_gain, expert_gain, conv_weight, conv_bias):
    rows, cols, width = tokens.shape
    size = rows * cols * width
    message = (4 * slots * holders, width // 2)
    return pl.pallas_call(
        functools.partial(mix_kernel, holders, slots),
        out_shape=[
            jax.ShapeDtypeStruct((rows * cols, width), jnp.float32),
            jax.ShapeDtypeStruct(message, jnp.bfloat16),
            jax.ShapeDtypeStruct((2, rows * cols), jnp.int32),
        ],
        in_specs=[VMEM] * 8,
        out_specs=[HBM, HBM, VMEM],
        scratch_shapes=[
            pltpu.VMEM((rows + 2, cols, width), jnp.bfloat16),
            pltpu.VMEM((rows * cols, width), jnp.bfloat16),
            pltpu.VMEM((rows * cols, width), jnp.float32),
            pltpu.VMEM(message, jnp.bfloat16),
            pltpu.SemaphoreType.DMA((2,)),
        ],
        compiler_params=pltpu.CompilerParams(vmem_limit_bytes=16 * 1024 * 1024),
        cost_estimate=pl.CostEstimate(flops=MIX_COST * size, transcendentals=0, bytes_accessed=6 * size),
        name="mix",
    )(tokens, up, down, ids, mixer_gain, expert_gain, conv_weight, conv_bias)


def ffn_kernel(*refs):
    msgs, wis, wos = refs[0:4], refs[4:8], refs[8:12]
    bias, pick, place_first, place_second = refs[12:16]
    outs, refs = (refs[16:20], refs[20:24]), refs[24:]
    r_v, x_v, wi_v, wo_v, y_first, y_second, o_first, o_second, msg_sem, w_sem, out_sem = refs
    experts, total, width = x_v.shape
    rows = total // SIDE
    units = wos[0].shape[1]
    half = width // 2
    places, ys, os = (place_first, place_second), (y_first, y_second), (o_first, o_second)
    sizes = [y.shape[1] // experts for y in ys]
    msg_copies = []
    for k in range(SIDE):
        copy = pltpu.make_async_copy(msgs[k], r_v.at[k], msg_sem.at[k])
        copy.start()
        msg_copies.append(copy)
    w_copies = {}
    for j in range(experts):
        for what, (sources, target) in enumerate(((wis, wi_v), (wos, wo_v))):
            group = []
            for k in range(SIDE):
                copy = pltpu.make_async_copy(
                    sources[k].at[j], target.at[j, pl.ds(k * units, units)], w_sem.at[j, what, k]
                )
                copy.start()
                group.append(copy)
            w_copies[j, what] = group
    for k in range(SIDE):
        msg_copies[k].wait()
        for side in range(2):
            found = jnp.dot(pick[side], r_v[k], preferred_element_type=jnp.float32).astype(
                jnp.bfloat16
            )
            row = 0
            for j in range(experts):
                base = 0
                for size in sizes:
                    x_v[
                        j,
                        base + k * size : base + (k + 1) * size,
                        side * half : (side + 1) * half,
                    ] = found[row : row + size]
                    row += size
                    base += SIDE * size
    for j in range(experts):
        for copy in w_copies[j, 0]:
            copy.wait()
        base = 0
        for c, size in enumerate(sizes):
            at = slice(base, base + SIDE * size)
            base += SIDE * size
            hidden = lax.dot_general(
                x_v[j, at], wi_v[j], (((1,), (1,)), ((), ())), preferred_element_type=jnp.float32
            )
            hidden = gelu(hidden + bias[j : j + 1]).astype(jnp.bfloat16)
            if c == 0:
                for copy in w_copies[j, 1]:
                    copy.wait()
            part = jnp.dot(hidden, wo_v[j], preferred_element_type=jnp.float32)
            part = part.astype(jnp.bfloat16)
            for k in range(SIDE):
                ys[c][k, j * size : (j + 1) * size] = part[k * size : (k + 1) * size]
            if j == experts - 1:
                for k in range(SIDE):
                    os[c][k] = (
                        jnp.dot(places[c][0], ys[c][k, :, :half], preferred_element_type=jnp.float32)
                        + jnp.dot(
                            places[c][1], ys[c][k, :, half:], preferred_element_type=jnp.float32
                        )
                    ).astype(jnp.bfloat16)
                    copy = pltpu.make_async_copy(os[c].at[k], outs[c][k], out_sem.at[c, k])
                    copy.start()
    for c in range(2):
        for k in range(SIDE):
            pltpu.make_async_copy(os[c].at[k], outs[c][k], out_sem.at[c, k]).wait()


def ffn(msgs, wis, wos, bias, pick, places):
    experts, units, width = wos[0].shape
    rows = pick.shape[1] // experts
    total = SIDE * rows
    shapes = [(place.shape[1], width // 2) for place in places]
    flops = 4 * experts * total * SIDE * units * width
    moved = 2 * experts * width * (4 * total + 2 * SIDE * units)
    outs = pl.pallas_call(
        ffn_kernel,
        out_shape=[
            jax.ShapeDtypeStruct(shape, jnp.bfloat16) for shape in shapes for _ in range(SIDE)
        ],
        in_specs=[ANY] * 12 + [VMEM] * 4,
        out_specs=[ANY] * (2 * SIDE),
        scratch_shapes=[
            pltpu.VMEM((SIDE,) + msgs[0].shape, jnp.bfloat16),
            pltpu.VMEM((experts, total, width), jnp.bfloat16),
            pltpu.VMEM((experts, SIDE * units, width), jnp.bfloat16),
            pltpu.VMEM((experts, SIDE * units, width), jnp.bfloat16),
            pltpu.VMEM((SIDE, places[0].shape[2], width), jnp.bfloat16),
            pltpu.VMEM((SIDE, places[1].shape[2], width), jnp.bfloat16),
            pltpu.VMEM((SIDE,) + shapes[0], jnp.bfloat16),
            pltpu.VMEM((SIDE,) + shapes[1], jnp.bfloat16),
            pltpu.SemaphoreType.DMA((SIDE,)),
            pltpu.SemaphoreType.DMA((experts, 2, SIDE)),
            pltpu.SemaphoreType.DMA((2, SIDE)),
        ],
        compiler_params=pltpu.CompilerParams(vmem_limit_bytes=40 * 1024 * 1024),
        cost_estimate=pl.CostEstimate(flops=2 * flops, transcendentals=0, bytes_accessed=moved),
        name="ffn",
    )(*msgs, *wis, *wos, bias, pick, *places)
    return outs[:SIDE], outs[SIDE:]


def combine_kernel(mixed_ref, gate_ref, col_ref, first_ref, second_ref, out_ref):
    tokens, width = mixed_ref.shape
    gate = gate_ref[...]
    for side in range(2):
        at = slice(side * width // 2, (side + 1) * width // 2)
        total = None
        for k, ref in enumerate((first_ref, second_ref)):
            count = ref.shape[0]
            step = 2 * (count // 64) * side
            col = col_ref[:, k : k + 1] + step
            pick = lax.broadcasted_iota(jnp.int32, (tokens, count), 1) == col
            term = jnp.dot(
                pick.astype(jnp.float32).astype(jnp.bfloat16),
                ref[...],
                preferred_element_type=jnp.float32,
            )
            total = term if total is None else total + term
        out_ref[:, at] = (mixed_ref[:, at] + gate * total).astype(jnp.bfloat16)


def combine(mixed, gate, columns, first, second):
    return pl.pallas_call(
        combine_kernel,
        out_shape=jax.ShapeDtypeStruct(mixed.shape, jnp.bfloat16),
        in_specs=[VMEM] * 5,
        out_specs=VMEM,
        compiler_params=pltpu.CompilerParams(vmem_limit_bytes=16 * 1024 * 1024),
        name="combine",
    )(mixed, gate, columns, first, second)


def body(
    tokens,
    expert_ids,
    gate_values,
    mixer_gain,
    expert_gain,
    conv_weight,
    conv_bias,
    w_in,
    b_in,
    w_out,
    b_out,
):
    exp_size = lax.axis_size("exp")
    seq_size = lax.axis_size("seq")
    send_w = functools.partial(ring, weights=True, exp_size=exp_size)
    send_t = functools.partial(ring, weights=False, exp_size=exp_size)
    _, row_count, col_count, width = tokens.shape
    tok_rows = row_count * col_count
    per_device = w_in.shape[0]
    slots = 5 * tok_rows // (4 * per_device * exp_size)

    together = lax.optimization_barrier
    head, tail = tokens[0, 0:1], tokens[0, row_count - 1 : row_count]
    wi, wo = jnp.swapaxes(w_in, 1, 2), w_out
    up = lax.ppermute(tail, "seq", [(i, i + 1) for i in range(seq_size - 1)])
    down = lax.ppermute(head, "seq", [(i + 1, i) for i in range(seq_size - 1)])
    wi_prev = lax.ppermute(wi, AXES, send_w(1))
    wi_next = lax.ppermute(wi, AXES, send_w(-1))
    wo_prev = lax.ppermute(wo, AXES, send_w(1))
    wo_next = lax.ppermute(wo, AXES, send_w(-1))
    mixed, msg, columns = mix(
        exp_size,
        slots,
        tokens[0],
        up,
        down,
        expert_ids.reshape(1, tok_rows),
        mixer_gain,
        expert_gain,
        conv_weight,
        conv_bias,
    )

    def exchange(msg):
        shape = msg.shape
        msg = msg.reshape(exp_size, shape[0] // exp_size, shape[1])
        return lax.all_to_all(msg, "exp", split_axis=0, concat_axis=0, tiled=True).reshape(shape)

    def returned(parts, n):
        own, far, prev, nxt = parts
        far = lax.ppermute(far, AXES, send_t(2))
        prev = lax.ppermute(prev, AXES, send_t(-1))
        nxt = lax.ppermute(nxt, AXES, send_t(1))
        shift = jnp.transpose(b_out.reshape(per_device, 2, width // 2), (1, 0, 2))
        shift = jnp.broadcast_to(shift[None, :, :, None], (exp_size, 2, per_device, n, width // 2))
        total = sum(part.astype(jnp.float32) for part in (own, far, prev, nxt))
        return (total + shift.reshape(total.shape)).astype(jnp.bfloat16)

    msg = exchange(msg)
    msg_far = lax.ppermute(msg, AXES, send_t(2))
    msg_prev = lax.ppermute(msg, AXES, send_t(1))
    msg_next = lax.ppermute(msg, AXES, send_t(-1))
    wi_on, wo_on, bias_in, _ = together((wi_prev, wo_next, b_in, msg))
    wi_far = lax.ppermute(wi_on, AXES, send_w(1))
    wo_far = lax.ppermute(wo_on, AXES, send_w(-1))
    biases = lax.all_gather(bias_in, AXES, axis_index_groups=weight_groups(exp_size))
    seq = lax.axis_index("seq")
    place = jnp.where(lax.axis_index("exp") % 2 == 0, seq % SIDE, seq // SIDE)
    bias = jnp.concatenate(
        [
            sum(jnp.where((place + shift) % SIDE == k, biases[k], 0.0) for k in range(SIDE))
            for shift in (0, SIDE - 1, 1, 2)
        ],
        axis=1,
    )
    sizes = chunk_sizes(slots)
    first, second = ffn(
        (msg, msg_far, msg_prev, msg_next),
        (wi, wi_prev, wi_next, wi_far),
        (wo, wo_prev, wo_next, wo_far),
        bias,
        unpack_table(exp_size, slots),
        [pack_table(exp_size, n) for n in sizes],
    )
    first = exchange(returned(first, sizes[0]))
    second, first = together((returned(second, sizes[1]), first))
    second = exchange(second)
    result = combine(mixed, gate_values.reshape(tok_rows, 1), columns.T, first, second)
    return result.reshape(tokens.shape)


def solution(mesh):
    in_specs = (
        P(("dp", "exp"), "seq", None, None),
        P(("dp", "exp"), "seq", None, None),
        P(("dp", "exp"), "seq", None),
        P(),
        P(),
        P(),
        P(),
        P("exp", None, "seq"),
        P("exp", "seq"),
        P("exp", "seq", None),
        P("exp", None),
    )
    out_specs = P(("dp", "exp"), "seq", None, None)
    return jax.shard_map(body, mesh=mesh, in_specs=in_specs, out_specs=out_specs, check_vma=False)
```

```python
import functools
import jax
import jax.numpy as jnp
import numpy as np
from jax import lax
from jax.experimental import pallas as pl
from jax.experimental.pallas import tpu as pltpu
from jax.sharding import PartitionSpec as P

SIDE = 4
AXES = ("seq", "exp")
VMEM = pl.BlockSpec(memory_space=pltpu.VMEM)
ANY = pl.BlockSpec(memory_space=pl.ANY)
HBM = pl.BlockSpec(memory_space=pltpu.HBM)
PIECES = 3
MIX_COST = 60000
FFN_COST = 2
ADD_COST = 64000
EXTRA = 16


def ring(shift, weights, exp_size):
    pairs = []
    for y in range(SIDE):
        for x in range(SIDE):
            for e in range(exp_size):
                along_x = (e % 2 == 0) == weights
                to_y = y if along_x else (y + shift) % SIDE
                to_x = (x + shift) % SIDE if along_x else x
                pairs.append(((y * SIDE + x) * exp_size + e, (to_y * SIDE + to_x) * exp_size + e))
    return pairs


def tables(holders, slots):
    pick = np.zeros((2, 2 * holders * slots, 4 * holders * slots), np.float32)
    for half in range(2):
        for j in range(2):
            for s in range(holders):
                for c in range(slots):
                    row = (j * holders + s) * slots + c
                    pick[half, row, s * 4 * slots + half * 2 * slots + j * slots + c] = 1.0
    return pick.astype(jnp.bfloat16), np.swapaxes(pick, 1, 2).astype(jnp.bfloat16)


def append_kernel(wi_ref, bias_ref, out_ref, rows_v, sems):
    experts, units, width = wi_ref.shape
    copies = []
    for j in range(experts):
        copy = pltpu.make_async_copy(wi_ref.at[j], out_ref.at[j, pl.ds(0, units)], sems.at[j])
        copy.start()
        copies.append(copy)
    rows_v[...] = jnp.zeros_like(rows_v)
    for j in range(experts):
        rows_v[j, 0:1, 0:units] = bias_ref[j : j + 1]
    for j in range(experts):
        left = rows_v[j, 0:1]
        for p in range(PIECES):
            piece = left.astype(jnp.bfloat16).astype(jnp.float32)
            left = left - piece
            for k in range(SIDE):
                row = PIECES * k + p
                rows_v[j, row : row + 1] = pltpu.roll(piece, k * units, 1) if k else piece
        out_ref[j, units : units + EXTRA] = rows_v[j].astype(jnp.bfloat16)
    for copy in copies:
        copy.wait()


def append_rows(wi, bias):
    experts, units, width = wi.shape
    return pl.pallas_call(
        append_kernel,
        out_shape=jax.ShapeDtypeStruct((experts, units + EXTRA, width), jnp.bfloat16),
        in_specs=[ANY, VMEM],
        out_specs=VMEM,
        scratch_shapes=[
            pltpu.VMEM((experts, EXTRA, width), jnp.float32),
            pltpu.SemaphoreType.DMA((experts,)),
        ],
        compiler_params=pltpu.CompilerParams(vmem_limit_bytes=8 * 1024 * 1024),
        name="append_rows",
    )(wi, bias)


def normalize(values, scales):
    row_mean = jnp.mean(values, axis=-1, keepdims=True)
    centred = values - row_mean
    row_var = jnp.mean(centred * centred, axis=-1, keepdims=True)
    return centred * lax.rsqrt(row_var + 1e-06) * scales


def gelu(v):
    return 0.5 * v * (1.0 + lax.erf(v * 0.7071067811865476))


def mix_kernel(
    holders,
    slots,
    tok_ref,
    up_ref,
    down_ref,
    ids_ref,
    mixer_gain,
    expert_gain,
    conv_weight,
    conv_bias,
    mixed_ref,
    msg_ref,
    column_ref,
    norm_v,
    in_v,
    mixed_v,
    msg_v,
    sems,
):
    rows, cols, width = tok_ref.shape
    tokens = rows * cols
    gain = mixer_gain[...].reshape(1, width)
    out_gain = expert_gain[...].reshape(1, width)
    shift = conv_bias[...].reshape(1, width)
    for r in range(rows):
        norm_v[r + 1] = normalize(tok_ref[r].astype(jnp.float32), gain).astype(jnp.bfloat16)
    norm_v[0] = normalize(up_ref[0].astype(jnp.float32), gain).astype(jnp.bfloat16)
    norm_v[rows + 1] = normalize(down_ref[0].astype(jnp.float32), gain).astype(jnp.bfloat16)
    place = lax.broadcasted_iota(jnp.int32, (cols, 1), 0)
    copies = []
    for r in range(rows):
        sums = []
        for b in range(3):
            total = None
            for a in range(3):
                term = norm_v[r + a].astype(jnp.float32) * conv_weight[a, b : b + 1]
                total = term if total is None else total + term
            sums.append(total)
        left = jnp.where(place == 0, 0.0, pltpu.roll(sums[0], 1, 0))
        right = jnp.where(place == cols - 1, 0.0, pltpu.roll(sums[2], cols - 1, 0))
        mixed = tok_ref[r].astype(jnp.float32) + shift + sums[1] + left + right
        at = pl.ds(r * cols, cols)
        mixed_v[at] = mixed
        in_v[at] = normalize(mixed, out_gain).astype(jnp.bfloat16)
    copies.append(pltpu.make_async_copy(mixed_v, mixed_ref, sems.at[0]))
    copies[0].start()
    ids = ids_ref[...]
    experts = 2 * holders
    kinds = lax.broadcasted_iota(jnp.int32, (experts, tokens), 0)
    hot = kinds == ids
    before = lax.broadcasted_iota(jnp.int32, (tokens, tokens), 0) < lax.broadcasted_iota(
        jnp.int32, (tokens, tokens), 1
    )
    earlier = jnp.dot(
        hot.astype(jnp.float32).astype(jnp.bfloat16),
        before.astype(jnp.float32).astype(jnp.bfloat16),
        preferred_element_type=jnp.float32,
    )
    rank = jnp.sum(jnp.where(hot, earlier, 0.0), axis=0, keepdims=True).astype(jnp.int32)
    holder = lax.shift_right_logical(ids, 1)
    which = ids & 1
    col = holder * (4 * slots) + which * slots + rank
    column_ref[...] = col
    at = lax.broadcasted_iota(jnp.int32, (4 * slots * holders, tokens), 0)
    pick_left = (at == col).astype(jnp.float32).astype(jnp.bfloat16)
    pick_right = (at == col + 2 * slots).astype(jnp.float32).astype(jnp.bfloat16)
    msg_v[...] = (
        jnp.dot(pick_left, in_v[:, : width // 2], preferred_element_type=jnp.float32)
        + jnp.dot(pick_right, in_v[:, width // 2 :], preferred_element_type=jnp.float32)
    ).astype(jnp.bfloat16)
    copies.append(pltpu.make_async_copy(msg_v, msg_ref, sems.at[1]))
    copies[1].start()
    for copy in copies:
        copy.wait()


def mix(holders, slots, tokens, up, down, ids, mixer_gain, expert_gain, conv_weight, conv_bias):
    rows, cols, width = tokens.shape
    size = rows * cols * width
    message = (4 * slots * holders, width // 2)
    return pl.pallas_call(
        functools.partial(mix_kernel, holders, slots),
        out_shape=[
            jax.ShapeDtypeStruct((rows * cols, width), jnp.float32),
            jax.ShapeDtypeStruct(message, jnp.bfloat16),
            jax.ShapeDtypeStruct((1, rows * cols), jnp.int32),
        ],
        in_specs=[VMEM] * 8,
        out_specs=[HBM, HBM, VMEM],
        scratch_shapes=[
            pltpu.VMEM((rows + 2, cols, width), jnp.bfloat16),
            pltpu.VMEM((rows * cols, width), jnp.bfloat16),
            pltpu.VMEM((rows * cols, width), jnp.float32),
            pltpu.VMEM(message, jnp.bfloat16),
            pltpu.SemaphoreType.DMA((2,)),
        ],
        compiler_params=pltpu.CompilerParams(vmem_limit_bytes=16 * 1024 * 1024),
        cost_estimate=pl.CostEstimate(flops=MIX_COST * size, transcendentals=0, bytes_accessed=6 * size),
        name="mix",
    )(tokens, up, down, ids, mixer_gain, expert_gain, conv_weight, conv_bias)


def unpack_kernel(msg_ref, pick, *outs):
    rows, width = outs[0].shape
    half = width // 2
    for side in range(2):
        found = jnp.dot(pick[side], msg_ref[...], preferred_element_type=jnp.float32)
        for j, out_ref in enumerate(outs):
            out_ref[:, side * half : (side + 1) * half] = found[
                j * rows : (j + 1) * rows
            ].astype(jnp.bfloat16)


def unpack(msg, pick):
    rows = pick.shape[1] // 2
    return pl.pallas_call(
        unpack_kernel,
        out_shape=[jax.ShapeDtypeStruct((rows, 2 * msg.shape[1]), jnp.bfloat16)] * 2,
        in_specs=[VMEM] * 2,
        out_specs=[VMEM] * 2,
        compiler_params=pltpu.CompilerParams(vmem_limit_bytes=16 * 1024 * 1024),
        name="unpack",
    )(msg, pick)


def ffn_kernel(expert, *refs):
    xs, wis, wos, outs = refs[0:4], refs[4:8], refs[8:12], refs[12:16]
    x_v, wi_v, wo_v, b_v, y_v, x_sem, w_sem, out_sem = refs[16:]
    rows = xs[0].shape[0]
    units = wos[0].shape[1]
    first, second = [], []
    for k in range(SIDE):
        at = expert if k < SIDE - 1 else 0
        first.append(
            pltpu.make_async_copy(xs[k], x_v.at[pl.ds(k * rows, rows)], x_sem.at[k])
        )
        first.append(
            pltpu.make_async_copy(
                wis[k].at[at, pl.ds(0, units)], wi_v.at[pl.ds(k * units, units)], w_sem.at[0, k]
            )
        )
        first.append(
            pltpu.make_async_copy(
                wis[k].at[at, pl.ds(units, EXTRA)], b_v.at[k], w_sem.at[2, k]
            )
        )
        second.append(
            pltpu.make_async_copy(
                wos[k].at[at], wo_v.at[pl.ds(k * units, units)], w_sem.at[1, k]
            )
        )
    for copy in first + second:
        copy.start()
    for copy in first:
        copy.wait()
    bias = sum(
        jnp.sum(b_v[k].astype(jnp.float32)[PIECES * k : PIECES * (k + 1)], axis=0, keepdims=True)
        for k in range(SIDE)
    )
    top, low = slice(0, 2 * rows), slice(2 * rows, 4 * rows)
    nt = (((1,), (1,)), ((), ()))
    first_hidden = lax.dot_general(
        x_v[top], wi_v[...], nt, preferred_element_type=jnp.float32
    )
    for copy in second:
        copy.wait()
    next_hidden = lax.dot_general(x_v[low], wi_v[...], nt, preferred_element_type=jnp.float32)
    first_hidden = gelu(first_hidden + bias).astype(jnp.bfloat16)
    part = jnp.dot(first_hidden, wo_v[...], preferred_element_type=jnp.float32)
    next_hidden = gelu(next_hidden + bias).astype(jnp.bfloat16)
    next_part = jnp.dot(next_hidden, wo_v[...], preferred_element_type=jnp.float32)
    y_v[top] = part.astype(jnp.bfloat16)
    y_v[low] = next_part.astype(jnp.bfloat16)
    out_copies = []
    for k in range(SIDE):
        copy = pltpu.make_async_copy(y_v.at[pl.ds(k * rows, rows)], outs[k], out_sem.at[k])
        copy.start()
        out_copies.append(copy)
    for copy in out_copies:
        copy.wait()


def ffn(expert, xs, wis, wos):
    rows, width = xs[0].shape
    units = wos[0].shape[1]
    flops = 4 * SIDE * rows * SIDE * units * width
    moved = 2 * width * (2 * SIDE * rows + 2 * SIDE * units)
    return pl.pallas_call(
        functools.partial(ffn_kernel, expert),
        out_shape=[jax.ShapeDtypeStruct((rows, width), jnp.bfloat16)] * SIDE,
        in_specs=[ANY] * 12,
        out_specs=[ANY] * SIDE,
        scratch_shapes=[
            pltpu.VMEM((SIDE * rows, width), jnp.bfloat16),
            pltpu.VMEM((SIDE * units, width), jnp.bfloat16),
            pltpu.VMEM((SIDE * units, width), jnp.bfloat16),
            pltpu.VMEM((SIDE, EXTRA, width), jnp.bfloat16),
            pltpu.VMEM((SIDE * rows, width), jnp.bfloat16),
            pltpu.SemaphoreType.DMA((SIDE,)),
            pltpu.SemaphoreType.DMA((3, SIDE)),
            pltpu.SemaphoreType.DMA((SIDE,)),
        ],
        compiler_params=pltpu.CompilerParams(vmem_limit_bytes=20 * 1024 * 1024),
        cost_estimate=pl.CostEstimate(
            flops=FFN_COST * flops, transcendentals=0, bytes_accessed=moved
        ),
        name="ffn",
    )(*xs, *wis, *wos)


def add_kernel(bias, *refs):
    parts, out_ref = refs[:-1], refs[-1]
    total = sum(part[...].astype(jnp.float32) for part in parts)
    out_ref[...] = (total + bias[0:1]).astype(jnp.bfloat16)


def add_parts(bias, parts):
    size = parts[0].size
    return pl.pallas_call(
        add_kernel,
        out_shape=jax.ShapeDtypeStruct(parts[0].shape, jnp.bfloat16),
        in_specs=[VMEM] * (1 + len(parts)),
        out_specs=VMEM,
        compiler_params=pltpu.CompilerParams(vmem_limit_bytes=8 * 1024 * 1024),
        cost_estimate=pl.CostEstimate(
            flops=ADD_COST * size, transcendentals=0, bytes_accessed=10 * size
        ),
        name="add_parts",
    )(bias, *parts)


def pack_kernel(place, bias, done_ref, *refs):
    parts, out_ref, sum_v = refs[:-2], refs[-2], refs[-1]
    rows, width = parts[0].shape
    half = width // 2
    total = sum(part[...].astype(jnp.float32) for part in parts)
    sum_v[...] = (total + bias[1:2]).astype(jnp.bfloat16)
    out_ref[...] = sum(
        jnp.dot(place[side, :, low : low + rows], ref[:, at], preferred_element_type=jnp.float32)
        for side, at in enumerate((slice(0, half), slice(half, width)))
        for low, ref in ((0, done_ref), (rows, sum_v))
    ).astype(jnp.bfloat16)


def pack(place, bias, done, parts):
    rows, width = parts[0].shape
    return pl.pallas_call(
        pack_kernel,
        out_shape=jax.ShapeDtypeStruct((place.shape[1], width // 2), jnp.bfloat16),
        in_specs=[VMEM] * (3 + len(parts)),
        out_specs=VMEM,
        scratch_shapes=[pltpu.VMEM((rows, width), jnp.bfloat16)],
        compiler_params=pltpu.CompilerParams(vmem_limit_bytes=16 * 1024 * 1024),
        name="pack",
    )(place, bias, done, *parts)


def combine_kernel(mixed_ref, gate_ref, col_ref, msg_ref, out_ref):
    tokens, width = mixed_ref.shape
    gate = gate_ref[...]
    count = msg_ref.shape[0]
    step = count // 32
    at_col = lax.broadcasted_iota(jnp.int32, (tokens, count), 1)
    for side in range(2):
        at = slice(side * width // 2, (side + 1) * width // 2)
        pick = at_col == col_ref[...] + step * side
        picked = jnp.dot(
            pick.astype(jnp.float32).astype(jnp.bfloat16),
            msg_ref[...],
            preferred_element_type=jnp.float32,
        )
        out_ref[:, at] = (mixed_ref[:, at] + gate * picked).astype(jnp.bfloat16)


def combine(mixed, gate, columns, msg):
    return pl.pallas_call(
        combine_kernel,
        out_shape=jax.ShapeDtypeStruct(mixed.shape, jnp.bfloat16),
        in_specs=[VMEM] * 4,
        out_specs=VMEM,
        compiler_params=pltpu.CompilerParams(vmem_limit_bytes=16 * 1024 * 1024),
        name="combine",
    )(mixed, gate, columns, msg)


def body(
    tokens,
    expert_ids,
    gate_values,
    mixer_gain,
    expert_gain,
    conv_weight,
    conv_bias,
    w_in,
    b_in,
    w_out,
    b_out,
):
    exp_size = lax.axis_size("exp")
    seq_size = lax.axis_size("seq")
    send_w = functools.partial(ring, weights=True, exp_size=exp_size)
    send_t = functools.partial(ring, weights=False, exp_size=exp_size)
    _, row_count, col_count, width = tokens.shape
    tok_rows = row_count * col_count
    per_device = w_in.shape[0]
    slots = 5 * tok_rows // (4 * per_device * exp_size)

    together = lax.optimization_barrier
    head, tail = tokens[0, 0:1], tokens[0, row_count - 1 : row_count]
    wi = append_rows(jnp.swapaxes(w_in, 1, 2), b_in)
    wo = w_out
    up = lax.ppermute(tail, "seq", [(i, i + 1) for i in range(seq_size - 1)])
    down = lax.ppermute(head, "seq", [(i + 1, i) for i in range(seq_size - 1)])
    wo_prev = lax.ppermute(wo, AXES, send_w(1))
    wo_next = lax.ppermute(wo, AXES, send_w(-1))
    wi_prev = lax.ppermute(wi, AXES, send_w(1))
    wi_next = lax.ppermute(wi, AXES, send_w(-1))
    mixed, msg, columns = mix(
        exp_size,
        slots,
        tokens[0],
        up,
        down,
        expert_ids.reshape(1, tok_rows),
        mixer_gain,
        expert_gain,
        conv_weight,
        conv_bias,
    )
    columns, wo_on, wi_on, *_ = together((columns, wo_prev, wi_next, wo_next, wi_prev))
    wo_far_0 = lax.ppermute(wo_on[0:1], AXES, send_w(1))
    wi_far_0 = lax.ppermute(wi_on[0:1], AXES, send_w(-1))

    def exchange(msg):
        shape = msg.shape
        msg = msg.reshape(exp_size, shape[0] // exp_size, shape[1])
        return lax.all_to_all(msg, "exp", split_axis=0, concat_axis=0, tiled=True).reshape(shape)

    def spread(rows, forward):
        prev = lax.ppermute(rows, AXES, send_t(1))
        nxt = lax.ppermute(rows, AXES, send_t(-1))
        far = lax.ppermute(prev if forward else rows, AXES, send_t(1 if forward else 2))
        return far, prev, nxt, rows

    def returned(parts):
        far, prev, nxt, own = parts
        return (
            own,
            lax.ppermute(far, AXES, send_t(2)),
            lax.ppermute(prev, AXES, send_t(-1)),
            lax.ppermute(nxt, AXES, send_t(1)),
        )

    pick, place = tables(exp_size, slots)
    rows_0, rows_1 = unpack(exchange(msg), pick)
    rows_0 = spread(rows_0, True)
    rows_1, rows_0, wo_on, wi_on = together((rows_1, rows_0, wo_on, wi_on))
    wo_far_1 = lax.ppermute(wo_on[1:2], AXES, send_w(1))
    wi_far_1 = lax.ppermute(wi_on[1:2], AXES, send_w(-1))
    weights_0 = ((wi, wi_prev, wi_next, wi_far_0), (wo, wo_prev, wo_next, wo_far_0))
    weights_1 = ((wi, wi_prev, wi_next, wi_far_1), (wo, wo_prev, wo_next, wo_far_1))
    rows_1 = spread(rows_1, False)
    parts_0 = ffn(0, rows_0, *weights_0)
    rows_1, _ = together((rows_1, parts_0[0]))
    parts_1 = ffn(1, rows_1, *weights_1)
    early = add_parts(b_out, returned(parts_0))
    back = pack(place, b_out, early, returned(parts_1))
    back = exchange(back)
    result = combine(mixed, gate_values.reshape(tok_rows, 1), columns.reshape(tok_rows, 1), back)
    return result.reshape(tokens.shape)


def solution(mesh):
    in_specs = (
        P(("dp", "exp"), "seq", None, None),
        P(("dp", "exp"), "seq", None, None),
        P(("dp", "exp"), "seq", None),
        P(),
        P(),
        P(),
        P(),
        P("exp", None, "seq"),
        P("exp", "seq"),
        P("exp", "seq", None),
        P("exp", None),
    )
    out_specs = P(("dp", "exp"), "seq", None, None)
    return jax.shard_map(body, mesh=mesh, in_specs=in_specs, out_specs=out_specs, check_vma=False)
```

```python
import functools
import jax
import jax.numpy as jnp
import numpy as np
from jax import lax
from jax.experimental import pallas as pl
from jax.experimental.pallas import tpu as pltpu
from jax.sharding import PartitionSpec as P

SIDE = 4
AXES = ("seq", "exp")
VMEM = pl.BlockSpec(memory_space=pltpu.VMEM)
ANY = pl.BlockSpec(memory_space=pl.ANY)
HBM = pl.BlockSpec(memory_space=pltpu.HBM)
PIECES = 3
MIX_COST = 60000
FFN_COST = 2
ADD_COST = 64000
EXTRA = 16


def ring(shift, weights, exp_size):
    pairs = []
    for y in range(SIDE):
        for x in range(SIDE):
            for e in range(exp_size):
                along_x = (e % 2 == 0) == weights
                to_y = y if along_x else (y + shift) % SIDE
                to_x = (x + shift) % SIDE if along_x else x
                pairs.append(((y * SIDE + x) * exp_size + e, (to_y * SIDE + to_x) * exp_size + e))
    return pairs


def tables(holders, slots):
    pick = np.zeros((2, 2 * holders * slots, 4 * holders * slots), np.float32)
    for half in range(2):
        for j in range(2):
            for s in range(holders):
                for c in range(slots):
                    row = (j * holders + s) * slots + c
                    pick[half, row, s * 4 * slots + half * 2 * slots + j * slots + c] = 1.0
    return pick.astype(jnp.bfloat16), np.swapaxes(pick, 1, 2).astype(jnp.bfloat16)


def append_kernel(wi_ref, bias_ref, out_ref, rows_v, sems):
    experts, units, width = wi_ref.shape
    copies = []
    for j in range(experts):
        copy = pltpu.make_async_copy(wi_ref.at[j], out_ref.at[j, pl.ds(0, units)], sems.at[j])
        copy.start()
        copies.append(copy)
    rows_v[...] = jnp.zeros_like(rows_v)
    for j in range(experts):
        rows_v[j, 0:1, 0:units] = bias_ref[j : j + 1]
    for j in range(experts):
        left = rows_v[j, 0:1]
        for p in range(PIECES):
            piece = left.astype(jnp.bfloat16).astype(jnp.float32)
            left = left - piece
            for k in range(SIDE):
                row = PIECES * k + p
                rows_v[j, row : row + 1] = pltpu.roll(piece, k * units, 1) if k else piece
        out_ref[j, units : units + EXTRA] = rows_v[j].astype(jnp.bfloat16)
    for copy in copies:
        copy.wait()


def append_rows(wi, bias):
    experts, units, width = wi.shape
    return pl.pallas_call(
        append_kernel,
        out_shape=jax.ShapeDtypeStruct((experts, units + EXTRA, width), jnp.bfloat16),
        in_specs=[ANY, VMEM],
        out_specs=VMEM,
        scratch_shapes=[
            pltpu.VMEM((experts, EXTRA, width), jnp.float32),
            pltpu.SemaphoreType.DMA((experts,)),
        ],
        compiler_params=pltpu.CompilerParams(vmem_limit_bytes=8 * 1024 * 1024),
        name="append_rows",
    )(wi, bias)


def normalize(values, scales):
    row_mean = jnp.mean(values, axis=-1, keepdims=True)
    centred = values - row_mean
    row_var = jnp.mean(centred * centred, axis=-1, keepdims=True)
    return centred * lax.rsqrt(row_var + 1e-06) * scales


def gelu(v):
    return 0.5 * v * (1.0 + lax.erf(v * 0.7071067811865476))


def mix_kernel(
    holders,
    slots,
    tok_ref,
    up_ref,
    down_ref,
    ids_ref,
    mixer_gain,
    expert_gain,
    conv_weight,
    conv_bias,
    mixed_ref,
    msg_ref,
    column_ref,
    norm_v,
    in_v,
    mixed_v,
    msg_v,
    sems,
):
    rows, cols, width = tok_ref.shape
    tokens = rows * cols
    gain = mixer_gain[...].reshape(1, width)
    out_gain = expert_gain[...].reshape(1, width)
    shift = conv_bias[...].reshape(1, width)
    for r in range(rows):
        norm_v[r + 1] = normalize(tok_ref[r].astype(jnp.float32), gain).astype(jnp.bfloat16)
    norm_v[0] = normalize(up_ref[0].astype(jnp.float32), gain).astype(jnp.bfloat16)
    norm_v[rows + 1] = normalize(down_ref[0].astype(jnp.float32), gain).astype(jnp.bfloat16)
    place = lax.broadcasted_iota(jnp.int32, (cols, 1), 0)
    copies = []
    for r in range(rows):
        sums = []
        for b in range(3):
            total = None
            for a in range(3):
                term = norm_v[r + a].astype(jnp.float32) * conv_weight[a, b : b + 1]
                total = term if total is None else total + term
            sums.append(total)
        left = jnp.where(place == 0, 0.0, pltpu.roll(sums[0], 1, 0))
        right = jnp.where(place == cols - 1, 0.0, pltpu.roll(sums[2], cols - 1, 0))
        mixed = tok_ref[r].astype(jnp.float32) + shift + sums[1] + left + right
        at = pl.ds(r * cols, cols)
        mixed_v[at] = mixed
        in_v[at] = normalize(mixed, out_gain).astype(jnp.bfloat16)
    copies.append(pltpu.make_async_copy(mixed_v, mixed_ref, sems.at[0]))
    copies[0].start()
    ids = ids_ref[...]
    experts = 2 * holders
    kinds = lax.broadcasted_iota(jnp.int32, (experts, tokens), 0)
    hot = kinds == ids
    before = lax.broadcasted_iota(jnp.int32, (tokens, tokens), 0) < lax.broadcasted_iota(
        jnp.int32, (tokens, tokens), 1
    )
    earlier = jnp.dot(
        hot.astype(jnp.float32).astype(jnp.bfloat16),
        before.astype(jnp.float32).astype(jnp.bfloat16),
        preferred_element_type=jnp.float32,
    )
    rank = jnp.sum(jnp.where(hot, earlier, 0.0), axis=0, keepdims=True).astype(jnp.int32)
    holder = lax.shift_right_logical(ids, 1)
    which = ids & 1
    col = holder * (4 * slots) + which * slots + rank
    column_ref[...] = col
    at = lax.broadcasted_iota(jnp.int32, (4 * slots * holders, tokens), 0)
    pick_left = (at == col).astype(jnp.float32).astype(jnp.bfloat16)
    pick_right = (at == col + 2 * slots).astype(jnp.float32).astype(jnp.bfloat16)
    msg_v[...] = (
        jnp.dot(pick_left, in_v[:, : width // 2], preferred_element_type=jnp.float32)
        + jnp.dot(pick_right, in_v[:, width // 2 :], preferred_element_type=jnp.float32)
    ).astype(jnp.bfloat16)
    copies.append(pltpu.make_async_copy(msg_v, msg_ref, sems.at[1]))
    copies[1].start()
    for copy in copies:
        copy.wait()


def mix(holders, slots, tokens, up, down, ids, mixer_gain, expert_gain, conv_weight, conv_bias):
    rows, cols, width = tokens.shape
    size = rows * cols * width
    message = (4 * slots * holders, width // 2)
    return pl.pallas_call(
        functools.partial(mix_kernel, holders, slots),
        out_shape=[
            jax.ShapeDtypeStruct((rows * cols, width), jnp.float32),
            jax.ShapeDtypeStruct(message, jnp.bfloat16),
            jax.ShapeDtypeStruct((1, rows * cols), jnp.int32),
        ],
        in_specs=[VMEM] * 8,
        out_specs=[HBM, HBM, VMEM],
        scratch_shapes=[
            pltpu.VMEM((rows + 2, cols, width), jnp.bfloat16),
            pltpu.VMEM((rows * cols, width), jnp.bfloat16),
            pltpu.VMEM((rows * cols, width), jnp.float32),
            pltpu.VMEM(message, jnp.bfloat16),
            pltpu.SemaphoreType.DMA((2,)),
        ],
        compiler_params=pltpu.CompilerParams(vmem_limit_bytes=16 * 1024 * 1024),
        cost_estimate=pl.CostEstimate(flops=MIX_COST * size, transcendentals=0, bytes_accessed=6 * size),
        name="mix",
    )(tokens, up, down, ids, mixer_gain, expert_gain, conv_weight, conv_bias)


def unpack_kernel(msg_ref, pick, *outs):
    rows, width = outs[0].shape
    half = width // 2
    for side in range(2):
        found = jnp.dot(pick[side], msg_ref[...], preferred_element_type=jnp.float32)
        for j, out_ref in enumerate(outs):
            out_ref[:, side * half : (side + 1) * half] = found[
                j * rows : (j + 1) * rows
            ].astype(jnp.bfloat16)


def unpack(msg, pick):
    rows = pick.shape[1] // 2
    return pl.pallas_call(
        unpack_kernel,
        out_shape=[jax.ShapeDtypeStruct((rows, 2 * msg.shape[1]), jnp.bfloat16)] * 2,
        in_specs=[VMEM] * 2,
        out_specs=[VMEM] * 2,
        compiler_params=pltpu.CompilerParams(vmem_limit_bytes=16 * 1024 * 1024),
        name="unpack",
    )(msg, pick)


def ffn_kernel(expert, *refs):
    xs, wis, wos, outs = refs[0:4], refs[4:8], refs[8:12], refs[12:16]
    x_v, wi_v, wo_v, b_v, y_v, x_sem, w_sem, out_sem = refs[16:]
    rows = xs[0].shape[0]
    units = wos[0].shape[1]
    first, second = [], []
    for k in range(SIDE):
        first.append(
            pltpu.make_async_copy(xs[k], x_v.at[pl.ds(k * rows, rows)], x_sem.at[k])
        )
        first.append(
            pltpu.make_async_copy(
                wis[k].at[expert, pl.ds(0, units)], wi_v.at[pl.ds(k * units, units)], w_sem.at[0, k]
            )
        )
        first.append(
            pltpu.make_async_copy(
                wis[k].at[expert, pl.ds(units, EXTRA)], b_v.at[k], w_sem.at[2, k]
            )
        )
        second.append(
            pltpu.make_async_copy(
                wos[k].at[expert], wo_v.at[pl.ds(k * units, units)], w_sem.at[1, k]
            )
        )
    for copy in first + second:
        copy.start()
    for copy in first:
        copy.wait()
    bias = sum(
        jnp.sum(b_v[k].astype(jnp.float32)[PIECES * k : PIECES * (k + 1)], axis=0, keepdims=True)
        for k in range(SIDE)
    )
    top, low = slice(0, 2 * rows), slice(2 * rows, 4 * rows)
    nt = (((1,), (1,)), ((), ()))
    first_hidden = lax.dot_general(
        x_v[top], wi_v[...], nt, preferred_element_type=jnp.float32
    )
    for copy in second:
        copy.wait()
    next_hidden = lax.dot_general(x_v[low], wi_v[...], nt, preferred_element_type=jnp.float32)
    first_hidden = gelu(first_hidden + bias).astype(jnp.bfloat16)
    part = jnp.dot(first_hidden, wo_v[...], preferred_element_type=jnp.float32)
    next_hidden = gelu(next_hidden + bias).astype(jnp.bfloat16)
    next_part = jnp.dot(next_hidden, wo_v[...], preferred_element_type=jnp.float32)
    y_v[top] = part.astype(jnp.bfloat16)
    y_v[low] = next_part.astype(jnp.bfloat16)
    out_copies = []
    for k in range(SIDE):
        copy = pltpu.make_async_copy(y_v.at[pl.ds(k * rows, rows)], outs[k], out_sem.at[k])
        copy.start()
        out_copies.append(copy)
    for copy in out_copies:
        copy.wait()


def ffn(expert, xs, wis, wos):
    rows, width = xs[0].shape
    units = wos[0].shape[1]
    flops = 4 * SIDE * rows * SIDE * units * width
    moved = 2 * width * (2 * SIDE * rows + 2 * SIDE * units)
    return pl.pallas_call(
        functools.partial(ffn_kernel, expert),
        out_shape=[jax.ShapeDtypeStruct((rows, width), jnp.bfloat16)] * SIDE,
        in_specs=[ANY] * 12,
        out_specs=[ANY] * SIDE,
        scratch_shapes=[
            pltpu.VMEM((SIDE * rows, width), jnp.bfloat16),
            pltpu.VMEM((SIDE * units, width), jnp.bfloat16),
            pltpu.VMEM((SIDE * units, width), jnp.bfloat16),
            pltpu.VMEM((SIDE, EXTRA, width), jnp.bfloat16),
            pltpu.VMEM((SIDE * rows, width), jnp.bfloat16),
            pltpu.SemaphoreType.DMA((SIDE,)),
            pltpu.SemaphoreType.DMA((3, SIDE)),
            pltpu.SemaphoreType.DMA((SIDE,)),
        ],
        compiler_params=pltpu.CompilerParams(vmem_limit_bytes=20 * 1024 * 1024),
        cost_estimate=pl.CostEstimate(
            flops=FFN_COST * flops, transcendentals=0, bytes_accessed=moved
        ),
        name="ffn",
    )(*xs, *wis, *wos)


def add_kernel(bias, *refs):
    parts, out_ref = refs[:-1], refs[-1]
    total = sum(part[...].astype(jnp.float32) for part in parts)
    out_ref[...] = (total + bias[0:1]).astype(jnp.bfloat16)


def add_parts(bias, parts):
    size = parts[0].size
    return pl.pallas_call(
        add_kernel,
        out_shape=jax.ShapeDtypeStruct(parts[0].shape, jnp.bfloat16),
        in_specs=[VMEM] * (1 + len(parts)),
        out_specs=VMEM,
        compiler_params=pltpu.CompilerParams(vmem_limit_bytes=8 * 1024 * 1024),
        cost_estimate=pl.CostEstimate(
            flops=ADD_COST * size, transcendentals=0, bytes_accessed=10 * size
        ),
        name="add_parts",
    )(bias, *parts)


def pack_kernel(place, bias, done_ref, *refs):
    parts, out_ref, sum_v = refs[:-2], refs[-2], refs[-1]
    rows, width = parts[0].shape
    half = width // 2
    total = sum(part[...].astype(jnp.float32) for part in parts)
    sum_v[...] = (total + bias[1:2]).astype(jnp.bfloat16)
    out_ref[...] = sum(
        jnp.dot(place[side, :, low : low + rows], ref[:, at], preferred_element_type=jnp.float32)
        for side, at in enumerate((slice(0, half), slice(half, width)))
        for low, ref in ((0, done_ref), (rows, sum_v))
    ).astype(jnp.bfloat16)


def pack(place, bias, done, parts):
    rows, width = parts[0].shape
    return pl.pallas_call(
        pack_kernel,
        out_shape=jax.ShapeDtypeStruct((place.shape[1], width // 2), jnp.bfloat16),
        in_specs=[VMEM] * (3 + len(parts)),
        out_specs=VMEM,
        scratch_shapes=[pltpu.VMEM((rows, width), jnp.bfloat16)],
        compiler_params=pltpu.CompilerParams(vmem_limit_bytes=16 * 1024 * 1024),
        name="pack",
    )(place, bias, done, *parts)


def combine_kernel(mixed_ref, gate_ref, col_ref, msg_ref, out_ref):
    tokens, width = mixed_ref.shape
    gate = gate_ref[...]
    count = msg_ref.shape[0]
    step = count // 32
    at_col = lax.broadcasted_iota(jnp.int32, (tokens, count), 1)
    for side in range(2):
        at = slice(side * width // 2, (side + 1) * width // 2)
        pick = at_col == col_ref[...] + step * side
        picked = jnp.dot(
            pick.astype(jnp.float32).astype(jnp.bfloat16),
            msg_ref[...],
            preferred_element_type=jnp.float32,
        )
        out_ref[:, at] = (mixed_ref[:, at] + gate * picked).astype(jnp.bfloat16)


def combine(mixed, gate, columns, msg):
    return pl.pallas_call(
        combine_kernel,
        out_shape=jax.ShapeDtypeStruct(mixed.shape, jnp.bfloat16),
        in_specs=[VMEM] * 4,
        out_specs=VMEM,
        compiler_params=pltpu.CompilerParams(vmem_limit_bytes=16 * 1024 * 1024),
        name="combine",
    )(mixed, gate, columns, msg)


def body(
    tokens,
    expert_ids,
    gate_values,
    mixer_gain,
    expert_gain,
    conv_weight,
    conv_bias,
    w_in,
    b_in,
    w_out,
    b_out,
):
    exp_size = lax.axis_size("exp")
    seq_size = lax.axis_size("seq")
    send_w = functools.partial(ring, weights=True, exp_size=exp_size)
    send_t = functools.partial(ring, weights=False, exp_size=exp_size)
    _, row_count, col_count, width = tokens.shape
    tok_rows = row_count * col_count
    per_device = w_in.shape[0]
    slots = 5 * tok_rows // (4 * per_device * exp_size)

    together = lax.optimization_barrier
    head, tail = tokens[0, 0:1], tokens[0, row_count - 1 : row_count]
    wi = append_rows(jnp.swapaxes(w_in, 1, 2), b_in)
    wo = w_out
    up = lax.ppermute(tail, "seq", [(i, i + 1) for i in range(seq_size - 1)])
    down = lax.ppermute(head, "seq", [(i + 1, i) for i in range(seq_size - 1)])
    wo_prev = lax.ppermute(wo, AXES, send_w(1))
    wo_next = lax.ppermute(wo, AXES, send_w(-1))
    wi_prev = lax.ppermute(wi, AXES, send_w(1))
    wi_next = lax.ppermute(wi, AXES, send_w(-1))
    mixed, msg, columns = mix(
        exp_size,
        slots,
        tokens[0],
        up,
        down,
        expert_ids.reshape(1, tok_rows),
        mixer_gain,
        expert_gain,
        conv_weight,
        conv_bias,
    )
    columns, wo_on, wi_on, *_ = together((columns, wo_prev, wi_next, wo_next, wi_prev))
    wo_far = lax.ppermute(wo_on, AXES, send_w(1))
    wi_far = lax.ppermute(wi_on, AXES, send_w(-1))

    def exchange(msg):
        shape = msg.shape
        msg = msg.reshape(exp_size, shape[0] // exp_size, shape[1])
        return lax.all_to_all(msg, "exp", split_axis=0, concat_axis=0, tiled=True).reshape(shape)

    def spread(rows, forward):
        prev = lax.ppermute(rows, AXES, send_t(1))
        nxt = lax.ppermute(rows, AXES, send_t(-1))
        far = lax.ppermute(prev if forward else rows, AXES, send_t(1 if forward else 2))
        return far, prev, nxt, rows

    def returned(parts):
        far, prev, nxt, own = parts
        return (
            own,
            lax.ppermute(far, AXES, send_t(2)),
            lax.ppermute(prev, AXES, send_t(-1)),
            lax.ppermute(nxt, AXES, send_t(1)),
        )

    pick, place = tables(exp_size, slots)
    rows_0, rows_1 = unpack(exchange(msg), pick)
    weights = ((wi, wi_prev, wi_next, wi_far), (wo, wo_prev, wo_next, wo_far))
    rows_0 = spread(rows_0, True)
    rows_1, rows_0, wi_far, wo_far = together((rows_1, rows_0, wi_far, wo_far))
    weights = ((wi, wi_prev, wi_next, wi_far), (wo, wo_prev, wo_next, wo_far))
    rows_1 = spread(rows_1, False)
    parts_0 = ffn(0, rows_0, *weights)
    rows_1, _ = together((rows_1, parts_0[0]))
    parts_1 = ffn(1, rows_1, *weights)
    early = add_parts(b_out, returned(parts_0))
    back = pack(place, b_out, early, returned(parts_1))
    back = exchange(back)
    result = combine(mixed, gate_values.reshape(tok_rows, 1), columns.reshape(tok_rows, 1), back)
    return result.reshape(tokens.shape)


def solution(mesh):
    in_specs = (
        P(("dp", "exp"), "seq", None, None),
        P(("dp", "exp"), "seq", None, None),
        P(("dp", "exp"), "seq", None),
        P(),
        P(),
        P(),
        P(),
        P("exp", None, "seq"),
        P("exp", "seq"),
        P("exp", "seq", None),
        P("exp", None),
    )
    out_specs = P(("dp", "exp"), "seq", None, None)
    return jax.shard_map(body, mesh=mesh, in_specs=in_specs, out_specs=out_specs, check_vma=False)
```
